512 devices in a mesh: slab: 128 (over z, x, y_lo), sec: 4 (over y_hi, core).
Axes of the slice: x: 4, y: 8 (y_hi: 2, y_lo: 4; y = y_hi * 4 + y_lo), z: 8, core: 2. Of those that a mesh axis runs over, the one named last changes fastest.
Arguments:
- displacement: float32 [5120, 4096], P('slab', 'sec'), may hold values from -6 to 6
- earlier_field: float32 [5120, 4096], P('slab', 'sec'), may hold values from -6 to 6
- region_ids: int32 [4096], P('sec'), may hold values from 0 to 7
- material: float32 [2, 8], replicated, may hold values from 0.5 to 1.5
- mode_shapes: float32 [4096, 64], P('sec'), may hold values from -0.75 to 0.75
- band_edges: int32 [2, 64], replicated, may hold values from 0 to 4095, as said below
Outputs:
- advanced_field: float32 [5120, 4096], P('slab', 'sec')
- band_field: bfloat16 [5120, 4096], P('slab', 'sec')
The draws below stay inside these ranges and needn't reach their ends.
Inputs may be any that keep to these rules, and one draw needn't show every extreme that they name: `band_edges`: for every mode the lower edge is below the upper edge; some mode's band starts at 0 and some mode's band ends at 4095.
All inputs are finite; a program needn't handle non-finite values.
Results may differ from the reference program's by a relative error of at most 0.001.
Values sent between devices are 32-bit elements; how exact they have to be, the bound alone decides.
A program may use at most 64 MiB of HBM per device.

```python
import math
import jax
import jax.numpy as jnp
from jax import lax

ROWS = 64
COLS = 64
MODES = 64
WAVES = 4096
REGIONS = 8
STEPS = 4
CELLS = 4096
PLANES = 5120


def draw_band_edges(key, part):
    first_key, second_key = jax.random.split(jax.random.fold_in(key, 7))
    lower_edge = jax.random.randint(first_key, (MODES,), 0, WAVES // 2)
    widths = jax.random.randint(second_key, (MODES,), WAVES // 8, WAVES // 2 + 1)
    upper_edge = lower_edge + widths
    positions = jnp.arange(MODES, dtype=jnp.int32)
    lower_edge = jnp.where(positions == 0, 0, lower_edge)
    upper_edge = jnp.where(positions == MODES - 1, WAVES - 1, upper_edge)
    return jnp.stack([lower_edge, upper_edge]).astype(jnp.int32)


def touch_ends(drawn, key, least, top_value):
    place = [jax.random.randint(jax.random.fold_in(key, axis), (), 0, length) for axis, length in enumerate(drawn.shape)]
    longest = drawn.shape.index(max(drawn.shape))
    next_to = place[:longest] + [(place[longest] + 1) % drawn.shape[longest]] + place[longest + 1:]
    return drawn.at[tuple(place)].set(least).at[tuple(next_to)].set(top_value)


def level_of(rng, shape, cuts, least, high):
    gain = 1.0
    for position, parts in cuts:
        heights = jax.random.uniform(jax.random.fold_in(jax.random.fold_in(rng, 6), position), (parts,), jnp.float32, least / len(cuts), high / len(cuts))
        gain = gain * jnp.repeat(jnp.exp(heights), shape[position] // parts).reshape((-1,) + (1,) * (len(shape) - 1 - position))
    return gain


def scatter_about(rng, extent, scale, reach, pieces=(), held_as=jnp.bfloat16):
    result = scale * jax.random.normal(rng, extent, jnp.float32)
    if pieces:
        result = result * level_of(rng, extent, pieces, -0.22, 0.18)
    return jnp.clip(result, -reach, reach).astype(held_as)


def setup_inputs(seed: int = 0) -> dict:
    streams_of = jax.random.split(jax.random.key(seed), 7)
    displacement = scatter_about(streams_of[0], (PLANES, CELLS), 1.0, 6.0, ((0, 128), (1, 4)), jnp.float32)
    earlier_field = scatter_about(streams_of[1], (PLANES, CELLS), 1.0, 6.0, ((0, 128), (1, 4)), jnp.float32)
    region_ids = touch_ends(jax.random.randint(streams_of[2], (CELLS,), 0, REGIONS), jax.random.fold_in(streams_of[2], 1), 0, REGIONS - 1).astype(jnp.int32)
    material = jnp.clip(jax.random.uniform(streams_of[3], (2, REGIONS), jnp.float32, 0.5, 1.5), 0.5, 1.5)
    mode_shapes = scatter_about(streams_of[4], (CELLS, MODES), 0.125, 0.75, ((0, 4),), jnp.float32)
    band_edges = draw_band_edges(jax.random.fold_in(streams_of[6], 71), 0)
    return dict(displacement=displacement, earlier_field=earlier_field, region_ids=region_ids, material=material, mode_shapes=mode_shapes, band_edges=band_edges)


courant_sq = 0.14
two_pi = 2.0 * math.pi


def lookup_stiffness(region_ids, material):
    values = courant_sq * material[0] * material[1]
    match = region_ids[:, None] == jnp.arange(REGIONS, dtype=jnp.int32)[None, :]
    return jnp.sum(jnp.where(match, values[None, :], jnp.zeros_like(values)[None, :]), axis=1)


def advance(current, before, stiffness):
    planar = current.reshape(PLANES, ROWS, COLS)
    padded = jnp.pad(planar, ((0, 0), (1, 1), (1, 1)))
    across = padded[:, :-2, 1:-1] + padded[:, 2:, 1:-1] + padded[:, 1:-1, :-2] + padded[:, 1:-1, 2:]
    summed = jnp.roll(current, 1, 0) + jnp.roll(current, -1, 0) + across.reshape(PLANES, CELLS)
    return 2.0 * current - before + stiffness[None, :] * (summed - 6.0 * current)


def phases(first, second):
    product = first[:, None] * second[None, :]
    return (product % PLANES).astype(jnp.float32) * (two_pi / PLANES)


def reference(displacement, earlier_field, region_ids, material, mode_shapes, band_edges):
    stiffness = lookup_stiffness(region_ids, material)
    current, before = displacement, earlier_field
    for _ in range(STEPS):
        current, before = advance(current, before, stiffness), current
    modal = jnp.dot(current, mode_shapes, precision=lax.Precision.HIGHEST)
    block_len = min(WAVES, 512)
    planes_all = jnp.arange(PLANES, dtype=jnp.int32)

    def forward(index):
        wavenums = index * block_len + jnp.arange(block_len, dtype=jnp.int32)
        angle = phases(wavenums, planes_all)
        return jnp.concatenate([jnp.dot(jnp.cos(angle), modal, precision=lax.Precision.HIGHEST),
                                jnp.dot(jnp.sin(angle), modal, precision=lax.Precision.HIGHEST)], axis=1)

    spectrum = lax.map(forward, jnp.arange(WAVES // block_len, dtype=jnp.int32)).reshape(WAVES, 2 * MODES)
    wavenums_all = jnp.arange(WAVES, dtype=jnp.int32)[:, None]
    lower_edge = jnp.concatenate([band_edges[0], band_edges[0]])[None, :]
    upper_edge = jnp.concatenate([band_edges[1], band_edges[1]])[None, :]
    in_band = (wavenums_all >= lower_edge) & (wavenums_all < upper_edge)
    filtered = jnp.where(in_band, spectrum, jnp.zeros_like(spectrum))
    portions = filtered.reshape(WAVES // block_len, block_len, 2 * MODES)

    def inverse(running, item):
        index, portion = item
        wavenums = index * block_len + jnp.arange(block_len, dtype=jnp.int32)
        angle = phases(planes_all, wavenums)
        running = running + jnp.dot(jnp.cos(angle), portion[:, :MODES], precision=lax.Precision.HIGHEST)
        running = running + jnp.dot(jnp.sin(angle), portion[:, MODES:], precision=lax.Precision.HIGHEST)
        return running, None

    smooth, _ = lax.scan(inverse, jnp.zeros((PLANES, MODES), jnp.float32),
                         (jnp.arange(WAVES // block_len, dtype=jnp.int32), portions))
    smooth = smooth * (2.0 / PLANES)
    band_field = jnp.dot(smooth, mode_shapes.T, precision=lax.Precision.HIGHEST).astype(jnp.bfloat16)
    return current, band_field
```

```python
import functools
import math

import jax
import jax.numpy as jnp
import numpy as np
from jax import lax
from jax.experimental import pallas as pl
from jax.experimental.pallas import tpu as pltpu
from jax.sharding import PartitionSpec as P

COLS = 64
MODES = 64
WAVES = 4096
REGIONS = 8
STEPS = 4
PLANES = 5120
SLABS = 128
SECS = 4
DEPTH = PLANES // SLABS
HALO = STEPS
PADB = 64
K1 = WAVES // SLABS
MODES_HERE = MODES // SECS
PAIRS = MODES_HERE // 2

courant_sq = 0.14
two_pi = 2.0 * math.pi
HIGHEST = lax.Precision.HIGHEST


def make_tables():
    k2 = np.arange(SLABS)
    first = two_pi * (np.outer(k2, k2) % SLABS) / SLABS
    dft_a = np.concatenate([np.cos(first), -np.sin(first)], axis=0)
    b = np.arange(PADB)
    live = (b < DEPTH).astype(np.float64)
    phi = two_pi * np.outer(k2, b) / PLANES
    tw_cos = np.tile(np.cos(phi) * live, (1, 2))
    tw_sin = np.tile(np.sin(phi) * live, (1, 2))
    psi = two_pi * (np.outer(b, np.arange(K1)) % DEPTH) / DEPTH
    pair = np.eye(2)
    c = np.kron(pair, np.cos(psi) * live[:, None])
    s = np.kron(pair, np.sin(psi) * live[:, None])
    forward = np.block([[c, -s], [s, c]])
    inverse = np.block([[c.T, s.T], [-s.T, c.T]])
    return [t.astype(np.float32) for t in (dft_a, tw_cos, tw_sin, forward, inverse)]


TABLES = make_tables()


def lookup_stiffness(region_ids, material):
    values = courant_sq * material[0] * material[1]
    match = region_ids[:, None] == jnp.arange(REGIONS, dtype=jnp.int32)[None, :]
    return jnp.sum(jnp.where(match, values[None, :], jnp.zeros_like(values)[None, :]), axis=1)


def advance_kernel(cur_ref, prev_ref, stiff_ref, shapes_ref, out_ref, modal_ref):
    current = cur_ref[...]
    before = prev_ref[...]
    planes, cells = current.shape
    stiff = stiff_ref[0:1, :]
    column = lax.broadcasted_iota(jnp.int32, (1, cells), 1) % COLS
    not_first = column > 0
    not_last = column < COLS - 1
    for _ in range(STEPS):
        west = jnp.where(not_first, pltpu.roll(current, 1, 1), 0.0)
        east = jnp.where(not_last, pltpu.roll(current, cells - 1, 1), 0.0)
        above = pltpu.roll(current, COLS, 1)
        below = pltpu.roll(current, cells - COLS, 1)
        prior = pltpu.roll(current, 1, 0)
        later = pltpu.roll(current, planes - 1, 0)
        summed = prior + later + above + below + west + east
        current, before = (
            2.0 * current - before + stiff * (summed - 6.0 * current),
            current,
        )
    edge = HALO * COLS
    final = current[HALO : planes - HALO, edge : cells - edge]
    out_ref[...] = final
    modal_ref[:, :DEPTH] = lax.dot_general(
        shapes_ref[...], final, (((1,), (1,)), ((), ())),
        precision=HIGHEST, preferred_element_type=jnp.float32,
    )
    modal_ref[:, DEPTH:] = jnp.zeros((MODES, PADB - DEPTH), jnp.float32)


def filter_kernel(
    x_ref, lower_ref, upper_ref, pc_ref, ps_ref, dft_ref, twc_ref, tws_ref, fwd_ref, inv_ref, out_ref
):
    dot = functools.partial(jnp.dot, precision=HIGHEST, preferred_element_type=jnp.float32)
    twc = twc_ref[...]
    tws = tws_ref[...]
    lanes = 2 * PADB
    row = lax.broadcasted_iota(jnp.int32, (SLABS, 4 * K1), 0)
    lane = lax.broadcasted_iota(jnp.int32, (SLABS, 4 * K1), 1)
    wave = row + SLABS * (lane % K1)
    for t in range(PAIRS):
        both = dot(dft_ref[...], x_ref[:, t * lanes : (t + 1) * lanes])
        real, imag = both[:SLABS], both[SLABS:]
        twisted = jnp.concatenate(
            [real * twc + imag * tws, imag * twc - real * tws], axis=1
        )
        spectrum = dot(twisted, fwd_ref[...])
        in_band = (wave >= lower_ref[t : t + 1, :]) & (wave < upper_ref[t : t + 1, :])
        filtered = jnp.where(in_band, spectrum, 0.0)
        back = dot(filtered, inv_ref[...])
        terms = back[:, :lanes] * pc_ref[...] - back[:, lanes:] * ps_ref[...]
        out_ref[t : t + 1, :] = jnp.sum(terms, axis=0, keepdims=True)


def shift_pair(last, leading, axis, peers, wrap):
    up = [(i, (i + 1) % peers) for i in range(peers if wrap else peers - 1)]
    down = [(j, i) for i, j in up]
    return lax.ppermute(last, axis, up), lax.ppermute(leading, axis, down)


def body(displacement, earlier_field, region_ids, material, mode_shapes, band_edges):
    cells = displacement.shape[1]
    stiffness = lookup_stiffness(region_ids, material)
    pile = jnp.concatenate(
        [displacement, earlier_field, jnp.broadcast_to(stiffness[None, :], (8, cells))], axis=0
    )
    edge = HALO * COLS
    before, after = shift_pair(pile[:, cells - edge :], pile[:, :edge], "sec", SECS, False)
    wide = jnp.concatenate([before, pile, after], axis=1)
    cur = wide[:DEPTH]
    prev = wide[DEPTH : 2 * DEPTH]
    stiff = wide[2 * DEPTH :]
    last = jnp.concatenate([cur[DEPTH - HALO :], prev[DEPTH - HALO :]], axis=0)
    leading = jnp.concatenate([cur[:HALO], prev[:HALO]], axis=0)
    before, after = shift_pair(last, leading, "slab", SLABS, True)
    cur = jnp.concatenate([before[:HALO], cur, after[:HALO]], axis=0)
    prev = jnp.concatenate([before[HALO:], prev, after[HALO:]], axis=0)
    shapes_t = mode_shapes.T
    current, modal_part = pl.pallas_call(
        advance_kernel,
        out_shape=(
            jax.ShapeDtypeStruct((DEPTH, cells), jnp.float32),
            jax.ShapeDtypeStruct((MODES, PADB), jnp.float32),
        ),
    )(cur, prev, stiff, shapes_t)
    modal = lax.psum_scatter(modal_part, "sec", scatter_dimension=0, tiled=True)
    x = lax.all_gather(modal.reshape(1, MODES_HERE * PADB), "slab", axis=0, tiled=True)

    slab = lax.axis_index("slab")
    k2 = jnp.arange(SLABS, dtype=jnp.int32)[:, None]
    lane_b = jnp.arange(2 * PADB, dtype=jnp.int32)[None, :] % PADB
    angle = ((k2 * (slab * DEPTH + lane_b)) % PLANES).astype(jnp.float32) * (two_pi / PLANES)
    pc = jnp.cos(angle) * (2.0 / PLANES)
    ps = jnp.sin(angle) * (2.0 / PLANES)
    edges = lax.dynamic_slice_in_dim(
        band_edges, lax.axis_index("sec") * MODES_HERE, MODES_HERE, axis=1
    )
    edges = jnp.broadcast_to(
        edges.reshape(2, PAIRS, 1, 2, 1), (2, PAIRS, 2, 2, K1)
    ).reshape(2, PAIRS, 4 * K1)
    smooth = pl.pallas_call(
        filter_kernel,
        out_shape=jax.ShapeDtypeStruct((PAIRS, 2 * PADB), jnp.float32),
    )(x, edges[0], edges[1], pc, ps, *[jnp.asarray(t) for t in TABLES])
    smooth = lax.all_gather(smooth.reshape(MODES_HERE, PADB), "sec", axis=0, tiled=True)
    band_field = lax.dot_general(
        smooth[:, :DEPTH], shapes_t, (((0,), (0,)), ((), ())),
        precision=HIGHEST, preferred_element_type=jnp.float32,
    ).astype(jnp.bfloat16)
    return current, band_field


def solution(mesh):
    return jax.shard_map(
        body,
        mesh=mesh,
        in_specs=(P("slab", "sec"), P("slab", "sec"), P("sec"), P(), P("sec", None), P()),
        out_specs=(P("slab", "sec"), P("slab", "sec")),
        check_vma=False,
    )
```

```python
import functools
import math

import jax
import jax.numpy as jnp
import numpy as np
from jax import lax
from jax.experimental import pallas as pl
from jax.experimental.pallas import tpu as pltpu
from jax.sharding import PartitionSpec as P

COLS = 64
MODES = 64
WAVES = 4096
REGIONS = 8
STEPS = 4
PLANES = 5120
SLABS = 128
SECS = 4
DEPTH = PLANES // SLABS
HALO = STEPS
PADB = 64
K1 = WAVES // SLABS
ZS = 8
PLACES = SLABS // ZS
GROUP = ZS * SECS
MESH = pl.DeviceIdType.MESH

courant_sq = 0.14
two_pi = 2.0 * math.pi
HIGHEST = lax.Precision.HIGHEST


def make_tables():
    k2 = np.arange(SLABS)
    held_a = (np.arange(ZS)[None, :] * PLACES + np.arange(PLACES)[:, None]).reshape(-1)
    first = two_pi * (np.outer(k2, held_a) % SLABS) / SLABS
    dft_a = np.concatenate([np.cos(first), -np.sin(first)], axis=0)
    b = np.arange(PADB)
    live = (b < DEPTH).astype(np.float64)
    phi = two_pi * np.outer(k2, b) / PLANES
    tw_cos = np.tile(np.cos(phi) * live, (1, 2))
    tw_sin = np.tile(np.sin(phi) * live, (1, 2))
    psi = two_pi * (np.outer(b, np.arange(K1)) % DEPTH) / DEPTH
    pair = np.eye(2)
    c = np.kron(pair, np.cos(psi) * live[:, None])
    s = np.kron(pair, np.sin(psi) * live[:, None])
    forward = np.block([[c, -s], [s, c]])
    inverse = np.block([[c.T, s.T], [-s.T, c.T]])
    return [t.astype(np.float32) for t in (dft_a, tw_cos, tw_sin, forward, inverse)]


TABLES = make_tables()


def lookup_stiffness(region_ids, material):
    values = courant_sq * material[0] * material[1]
    match = region_ids[:, None] == jnp.arange(REGIONS, dtype=jnp.int32)[None, :]
    return jnp.sum(jnp.where(match, values[None, :], jnp.zeros_like(values)[None, :]), axis=1)


def advance_kernel(cur_ref, prev_ref, stiff_ref, shapes_ref, out_ref, modal_ref):
    current = cur_ref[...]
    before = prev_ref[...]
    planes, cells = current.shape
    stiff = stiff_ref[0:1, :]
    column = lax.broadcasted_iota(jnp.int32, (1, cells), 1) % COLS
    not_first = column > 0
    not_last = column < COLS - 1
    for _ in range(STEPS):
        west = jnp.where(not_first, pltpu.roll(current, 1, 1), 0.0)
        east = jnp.where(not_last, pltpu.roll(current, cells - 1, 1), 0.0)
        above = pltpu.roll(current, COLS, 1)
        below = pltpu.roll(current, cells - COLS, 1)
        prior = pltpu.roll(current, 1, 0)
        later = pltpu.roll(current, planes - 1, 0)
        summed = prior + later + above + below + west + east
        current, before = (
            2.0 * current - before + stiff * (summed - 6.0 * current),
            current,
        )
    edge = HALO * COLS
    final = current[HALO : planes - HALO, edge : cells - edge]
    out_ref[...] = final
    modal_ref[:, :DEPTH] = lax.dot_general(
        shapes_ref[...], final, (((1,), (1,)), ((), ())),
        precision=HIGHEST, preferred_element_type=jnp.float32,
    )
    modal_ref[:, DEPTH:] = jnp.zeros((MODES, PADB - DEPTH), jnp.float32)


def filter_kernel(
    modal_ref, lower_ref, upper_ref, rows_ref, dft_ref, twc_ref, tws_ref, fwd_ref, inv_ref, out_ref,
    pieces, mine, held, sent, send1, recv1, send2, recv2, send3, recv3,
):
    slab = lax.axis_index("slab")
    sec = lax.axis_index("sec")
    z, place = slab // PLACES, slab % PLACES
    group = z * SECS + sec

    def in_group(step):
        other = lax.rem(group + step, GROUP)
        other_z = other // SECS
        return other, other_z, {"slab": other_z * PLACES + place, "sec": lax.rem(other, SECS)}

    def in_places(step):
        return {"slab": z * PLACES + lax.rem(place + step, PLACES), "sec": sec}

    barrier = pltpu.get_barrier_semaphore()

    @pl.loop(1, GROUP)
    def _(step):
        pl.semaphore_signal(barrier, inc=1, device_id=in_group(step)[2], device_id_type=MESH)

    @pl.loop(1, PLACES)
    def _(step):
        pl.semaphore_signal(barrier, inc=1, device_id=in_places(step), device_id_type=MESH)

    pl.semaphore_wait(barrier, GROUP + PLACES - 2)

    @pl.loop(1, GROUP)
    def _(step):
        other, _, device = in_group(step)
        pltpu.make_async_remote_copy(
            src_ref=modal_ref.at[other], dst_ref=pieces.at[group],
            send_sem=send1, recv_sem=recv1, device_id=device, device_id_type=MESH,
        ).start()

    pltpu.make_async_copy(modal_ref.at[group], pieces.at[group], recv1).start()
    pltpu.make_async_copy(pieces, pieces, recv1).wait()
    for i in range(ZS):
        total = pieces[SECS * i] + pieces[SECS * i + 1]
        total = total + pieces[SECS * i + 2] + pieces[SECS * i + 3]
        mine[i : i + 1, :] = total

    @pl.loop(1, PLACES)
    def _(step):
        pltpu.make_async_remote_copy(
            src_ref=mine, dst_ref=held.at[place],
            send_sem=send2, recv_sem=recv2, device_id=in_places(step), device_id_type=MESH,
        ).start()

    pltpu.make_async_copy(mine, held.at[place], recv2).start()
    pltpu.make_async_copy(held, held, recv2).wait()

    dot = functools.partial(jnp.dot, precision=HIGHEST, preferred_element_type=jnp.float32)
    lanes = 2 * PADB
    twc = twc_ref[...]
    tws = tws_ref[...]
    row = lax.broadcasted_iota(jnp.int32, (SLABS, 4 * K1), 0)
    lane = lax.broadcasted_iota(jnp.int32, (SLABS, 4 * K1), 1)
    wave = row + SLABS * (lane % K1)
    both = dot(dft_ref[...], held[...].reshape(SLABS, lanes))
    real, imag = both[:SLABS], both[SLABS:]
    twisted = jnp.concatenate([real * twc + imag * tws, imag * twc - real * tws], axis=1)
    spectrum = dot(twisted, fwd_ref[...])
    in_band = (wave >= lower_ref[...]) & (wave < upper_ref[...])
    filtered = jnp.where(in_band, spectrum, 0.0)
    back = dot(filtered, inv_ref[...])
    real, imag = back[:, :lanes], back[:, lanes:]
    twisted = jnp.concatenate([real * twc - imag * tws, imag * twc + real * tws], axis=0)
    smooth = dot(rows_ref[...], twisted)
    for i in range(ZS):
        sent[i] = smooth[i : i + 1, :]

    @pl.loop(1, GROUP)
    def _(step):
        _, other_z, device = in_group(step)
        pltpu.make_async_remote_copy(
            src_ref=sent.at[other_z], dst_ref=out_ref.at[group],
            send_sem=send3, recv_sem=recv3, device_id=device, device_id_type=MESH,
        ).start()

    pltpu.make_async_copy(sent.at[z], out_ref.at[group], recv3).start()
    pltpu.make_async_copy(out_ref, out_ref, recv3).wait()
    most = pieces.at[pl.ds(0, GROUP - 1)]
    pltpu.make_async_copy(most, most, send1).wait()
    most = held.at[pl.ds(0, PLACES - 1)]
    pltpu.make_async_copy(most, most, send2).wait()
    most = out_ref.at[pl.ds(0, GROUP - 1)]
    pltpu.make_async_copy(most, most, send3).wait()


def shift_pair(last, leading, axis, peers, wrap):
    up = [(i, (i + 1) % peers) for i in range(peers if wrap else peers - 1)]
    down = [(j, i) for i, j in up]
    return lax.ppermute(last, axis, up), lax.ppermute(leading, axis, down)


def body(displacement, earlier_field, region_ids, material, mode_shapes, band_edges):
    cells = displacement.shape[1]
    stiffness = lookup_stiffness(region_ids, material)
    pile = jnp.concatenate(
        [displacement, earlier_field, jnp.broadcast_to(stiffness[None, :], (8, cells))], axis=0
    )
    edge = HALO * COLS
    before, after = shift_pair(pile[:, cells - edge :], pile[:, :edge], "sec", SECS, False)
    wide = jnp.concatenate([before, pile, after], axis=1)
    cur = wide[:DEPTH]
    prev = wide[DEPTH : 2 * DEPTH]
    stiff = wide[2 * DEPTH :]
    last = jnp.concatenate([cur[DEPTH - HALO :], prev[DEPTH - HALO :]], axis=0)
    leading = jnp.concatenate([cur[:HALO], prev[:HALO]], axis=0)
    before, after = shift_pair(last, leading, "slab", SLABS, True)
    cur = jnp.concatenate([before[:HALO], cur, after[:HALO]], axis=0)
    prev = jnp.concatenate([before[HALO:], prev, after[HALO:]], axis=0)
    shapes_t = mode_shapes.T
    current, modal_part = pl.pallas_call(
        advance_kernel,
        out_shape=(
            jax.ShapeDtypeStruct((DEPTH, cells), jnp.float32),
            jax.ShapeDtypeStruct((MODES, PADB), jnp.float32),
        ),
    )(cur, prev, stiff, shapes_t)
    slab = lax.axis_index("slab")
    group = slab // PLACES * SECS + lax.axis_index("sec")
    k2 = jnp.arange(SLABS, dtype=jnp.int32)[None, :]
    places = jnp.arange(ZS, dtype=jnp.int32)[:, None] * PLACES + slab % PLACES
    angle = ((k2 * places) % SLABS).astype(jnp.float32) * (two_pi / SLABS)
    rows = jnp.concatenate([jnp.cos(angle), -jnp.sin(angle)], axis=1) * (2.0 / PLANES)
    edges = lax.dynamic_slice_in_dim(band_edges, group * 2, 2, axis=1)
    edges = jnp.broadcast_to(edges.reshape(2, 1, 2, 1), (2, 2, 2, K1)).reshape(2, 4 * K1)
    dma = pltpu.SemaphoreType.DMA
    smooth = pl.pallas_call(
        filter_kernel,
        out_shape=jax.ShapeDtypeStruct((GROUP, 1, 2 * PADB), jnp.float32),
        in_specs=[pl.BlockSpec(memory_space=pltpu.VMEM)] * 9,
        out_specs=pl.BlockSpec(memory_space=pltpu.VMEM),
        scratch_shapes=[
            pltpu.VMEM((GROUP, 1, 2 * PADB), jnp.float32),
            pltpu.VMEM((ZS, 2 * PADB), jnp.float32),
            pltpu.VMEM((PLACES, ZS, 2 * PADB), jnp.float32),
            pltpu.VMEM((ZS, 1, 2 * PADB), jnp.float32),
            dma, dma, dma, dma, dma, dma,
        ],
        compiler_params=pltpu.CompilerParams(collective_id=0, has_side_effects=True),
    )(
        modal_part.reshape(GROUP, 1, 2 * PADB), edges[0:1], edges[1:2], rows,
        *[jnp.asarray(t) for t in TABLES],
    )
    smooth = smooth.reshape(MODES, PADB)
    band_field = lax.dot_general(
        smooth[:, :DEPTH], shapes_t, (((0,), (0,)), ((), ())),
        precision=HIGHEST, preferred_element_type=jnp.float32,
    ).astype(jnp.bfloat16)
    return current, band_field


def solution(mesh):
    return jax.shard_map(
        body,
        mesh=mesh,
        in_specs=(P("slab", "sec"), P("slab", "sec"), P("sec"), P(), P("sec", None), P()),
        out_specs=(P("slab", "sec"), P("slab", "sec")),
        check_vma=False,
    )
```

```python
import functools
import math

import jax
import jax.numpy as jnp
import numpy as np
from jax import lax
from jax.experimental import pallas as pl
from jax.experimental.pallas import tpu as pltpu
from jax.sharding import PartitionSpec as P

COLS = 64
MODES = 64
WAVES = 4096
REGIONS = 8
STEPS = 4
PLANES = 5120
SLABS = 128
SECS = 4
DEPTH = PLANES // SLABS
PAD = 8
EDGE = STEPS * COLS
CELLS_HERE = 4096 // SECS
TALL = DEPTH + 2 * PAD
BROAD = CELLS_HERE + 2 * EDGE
BESIDE = ((0, 1), (0, -1), (1, 0), (-1, 0), (1, 1), (1, -1), (-1, 1), (-1, -1))
PADB = 64
K1 = WAVES // SLABS
ZS = 8
PLACES = SLABS // ZS
GROUP = ZS * SECS
MESH = pl.DeviceIdType.MESH

courant_sq = 0.14
two_pi = 2.0 * math.pi
HIGHEST = lax.Precision.HIGHEST


def make_tables():
    k2 = np.arange(SLABS)
    held_a = (np.arange(ZS)[None, :] * PLACES + np.arange(PLACES)[:, None]).reshape(-1)
    first = two_pi * (np.outer(k2, held_a) % SLABS) / SLABS
    dft_a = np.concatenate([np.cos(first), -np.sin(first)], axis=0)
    b = np.arange(PADB)
    live = (b < DEPTH).astype(np.float64)
    phi = two_pi * np.outer(k2, b) / PLANES
    tw_cos = np.tile(np.cos(phi) * live, (1, 2))
    tw_sin = np.tile(np.sin(phi) * live, (1, 2))
    psi = two_pi * (np.outer(b, np.arange(K1)) % DEPTH) / DEPTH
    pair = np.eye(2)
    c = np.kron(pair, np.cos(psi) * live[:, None])
    s = np.kron(pair, np.sin(psi) * live[:, None])
    forward = np.block([[c, -s], [s, c]])
    inverse = np.block([[c.T, s.T], [-s.T, c.T]])
    at = held_a.reshape(PLACES, ZS, 1) * k2
    last = two_pi * (at % SLABS) / SLABS
    rows = np.concatenate([np.cos(last), -np.sin(last)], axis=2) * (2.0 / PLANES)
    return [t.astype(np.float32) for t in (rows, dft_a, tw_cos, tw_sin, forward, inverse)]


TABLES = make_tables()


def rail_kernel(
    disp_ref, earlier_ref, region_ref, material_ref, edges_ref, shapes_ref,
    rows_ref, dft_ref, twc_ref, tws_ref, fwd_ref, inv_ref,
    out_ref, band_ref,
    stiff_ref, wide, modal_ref, pieces, mine, held, sent, smooth_ref,
    send0, recv0, send1, recv1, send2, recv2, send3, recv3,
):
    slab = lax.axis_index("slab")
    sec = lax.axis_index("sec")
    z, place = slab // PLACES, slab % PLACES
    group = z * SECS + sec

    def in_group(step):
        other = lax.rem(group + step, GROUP)
        other_z = other // SECS
        return other, other_z, {"slab": other_z * PLACES + place, "sec": lax.rem(other, SECS)}

    def in_places(step):
        return {"slab": z * PLACES + lax.rem(place + step, PLACES), "sec": sec}

    def beside(up, across):
        return {
            "slab": lax.rem(slab + (SLABS + up), SLABS),
            "sec": lax.rem(sec + (SECS + across), SECS),
        }

    barrier = pltpu.get_barrier_semaphore()

    @pl.loop(1, GROUP)
    def _(step):
        pl.semaphore_signal(barrier, inc=1, device_id=in_group(step)[2], device_id_type=MESH)

    @pl.loop(1, PLACES)
    def _(step):
        pl.semaphore_signal(barrier, inc=1, device_id=in_places(step), device_id_type=MESH)

    for up, across in BESIDE:
        pl.semaphore_signal(barrier, inc=1, device_id=beside(up, across), device_id_type=MESH)

    stiff = jnp.zeros((8, CELLS_HERE), jnp.float32)
    region = jnp.broadcast_to(region_ref[...], (8, CELLS_HERE))
    for r in range(REGIONS):
        value = courant_sq * material_ref[0, r] * material_ref[1, r]
        stiff = jnp.where(region == r, value, stiff)
    stiff_ref[...] = stiff

    pl.semaphore_wait(barrier, GROUP + PLACES - 2 + len(BESIDE))

    halo_copies = []

    def send_halo(src, base, src_rows, dst_rows, up, across):
        src_at, dst_at = {-1: (0, EDGE + CELLS_HERE), 1: (CELLS_HERE - EDGE, 0), 0: (0, EDGE)}[across]
        count = CELLS_HERE if across == 0 else EDGE
        src = src.at[pl.ds(*src_rows), pl.ds(src_at, count)]
        dst = wide.at[pl.ds(base + dst_rows, src_rows[1]), pl.ds(dst_at, count)]
        if up == 0 and across == 0:
            pltpu.make_async_copy(src, dst, recv0).start()
            return
        copy = pltpu.make_async_remote_copy(
            src_ref=src, dst_ref=dst, send_sem=send0.at[len(halo_copies)], recv_sem=recv0,
            device_id=beside(up, across), device_id_type=MESH,
        )
        copy.start()
        halo_copies.append(copy)

    for up, across in BESIDE + ((0, 0),):
        src_rows, dst_rows = {
            -1: ((0, PAD), PAD + DEPTH), 1: ((DEPTH - PAD, PAD), 0), 0: ((0, DEPTH), PAD)
        }[up]
        send_halo(disp_ref, 0, src_rows, dst_rows, up, across)
        send_halo(earlier_ref, TALL, src_rows, dst_rows, up, across)
        if up == 0:
            send_halo(stiff_ref, 2 * TALL, (0, PAD), 0, up, across)
    pltpu.make_async_copy(wide, wide, recv0).wait()

    lane = lax.broadcasted_iota(jnp.int32, (1, BROAD), 1)
    start = jnp.where(sec == 0, EDGE, 0)
    stop = jnp.where(sec == SECS - 1, EDGE + CELLS_HERE, BROAD)
    inside = (lane >= start) & (lane < stop)
    current = jnp.where(inside, wide[:TALL, :], 0.0)
    before = jnp.where(inside, wide[TALL : 2 * TALL, :], 0.0)
    stiff = jnp.where(inside, wide[2 * TALL : 2 * TALL + 1, :], 0.0)
    not_first = lane % COLS > 0
    not_last = lane % COLS < COLS - 1
    for _ in range(STEPS):
        west = jnp.where(not_first, pltpu.roll(current, 1, 1), 0.0)
        east = jnp.where(not_last, pltpu.roll(current, BROAD - 1, 1), 0.0)
        above = pltpu.roll(current, COLS, 1)
        below = pltpu.roll(current, BROAD - COLS, 1)
        prior = pltpu.roll(current, 1, 0)
        later = pltpu.roll(current, TALL - 1, 0)
        summed = prior + later + above + below + west + east
        current, before = (
            2.0 * current - before + stiff * (summed - 6.0 * current),
            current,
        )
    final = current[PAD : PAD + DEPTH, EDGE : EDGE + CELLS_HERE]
    out_ref[...] = final
    lanes = 2 * PADB
    front = shapes_ref[:GROUP, :]
    back_half = shapes_ref[GROUP:, :]

    def dot_rows(shapes, planes):
        return lax.dot_general(
            shapes, planes, (((1,), (1,)), ((), ())),
            precision=HIGHEST, preferred_element_type=jnp.float32,
        )

    def blank(count):
        return jnp.zeros((count, CELLS_HERE), jnp.float32)

    modal = dot_rows(front, jnp.concatenate([final, blank(lanes - DEPTH)], axis=0))
    modal = modal + dot_rows(
        back_half, jnp.concatenate([blank(PADB), final, blank(PADB - DEPTH)], axis=0)
    )
    for i in range(GROUP):
        modal_ref[i] = modal[i : i + 1, :]

    @pl.loop(1, GROUP)
    def _(step):
        other, _, device = in_group(step)
        pltpu.make_async_remote_copy(
            src_ref=modal_ref.at[other], dst_ref=pieces.at[group],
            send_sem=send1, recv_sem=recv1, device_id=device, device_id_type=MESH,
        ).start()

    pltpu.make_async_copy(modal_ref.at[group], pieces.at[group], recv1).start()
    pltpu.make_async_copy(pieces, pieces, recv1).wait()
    for i in range(ZS):
        total = pieces[SECS * i] + pieces[SECS * i + 1]
        total = total + pieces[SECS * i + 2] + pieces[SECS * i + 3]
        mine[i : i + 1, :] = total

    @pl.loop(1, PLACES)
    def _(step):
        pltpu.make_async_remote_copy(
            src_ref=mine, dst_ref=held.at[place],
            send_sem=send2, recv_sem=recv2, device_id=in_places(step), device_id_type=MESH,
        ).start()

    pltpu.make_async_copy(mine, held.at[place], recv2).start()
    pltpu.make_async_copy(held, held, recv2).wait()

    dot = functools.partial(jnp.dot, precision=HIGHEST, preferred_element_type=jnp.float32)
    twc = twc_ref[...]
    tws = tws_ref[...]
    row = lax.broadcasted_iota(jnp.int32, (SLABS, 4 * K1), 0)
    lane = lax.broadcasted_iota(jnp.int32, (SLABS, 4 * K1), 1)
    wave = row + SLABS * (lane % K1)
    is_front = lane % (2 * K1) < K1
    lower = jnp.where(is_front, edges_ref[0, group], edges_ref[0, group + GROUP])
    upper = jnp.where(is_front, edges_ref[1, group], edges_ref[1, group + GROUP])
    both = dot(dft_ref[...], held[...].reshape(SLABS, lanes))
    real, imag = both[:SLABS], both[SLABS:]
    twisted = jnp.concatenate([real * twc + imag * tws, imag * twc - real * tws], axis=1)
    spectrum = dot(twisted, fwd_ref[...])
    in_band = (wave >= lower) & (wave < upper)
    filtered = jnp.where(in_band, spectrum, 0.0)
    back = dot(filtered, inv_ref[...])
    real, imag = back[:, :lanes], back[:, lanes:]
    twisted = jnp.concatenate([real * twc - imag * tws, imag * twc + real * tws], axis=0)
    smooth = dot(rows_ref[place], twisted)
    for i in range(ZS):
        sent[i] = smooth[i : i + 1, :]

    @pl.loop(1, GROUP)
    def _(step):
        _, other_z, device = in_group(step)
        pltpu.make_async_remote_copy(
            src_ref=sent.at[other_z], dst_ref=smooth_ref.at[group],
            send_sem=send3, recv_sem=recv3, device_id=device, device_id_type=MESH,
        ).start()

    pltpu.make_async_copy(sent.at[z], smooth_ref.at[group], recv3).start()
    pltpu.make_async_copy(smooth_ref, smooth_ref, recv3).wait()
    gathered = smooth_ref[:, 0, :].T
    band = dot(gathered[:DEPTH], front) + dot(gathered[PADB : PADB + DEPTH], back_half)
    band_ref[...] = band.astype(jnp.bfloat16)
    for copy in halo_copies:
        copy.wait_send()
    most = pieces.at[pl.ds(0, GROUP - 1)]
    pltpu.make_async_copy(most, most, send1).wait()
    most = held.at[pl.ds(0, PLACES - 1)]
    pltpu.make_async_copy(most, most, send2).wait()
    most = smooth_ref.at[pl.ds(0, GROUP - 1)]
    pltpu.make_async_copy(most, most, send3).wait()


def body(displacement, earlier_field, region_ids, material, mode_shapes, band_edges):
    vmem = pl.BlockSpec(memory_space=pltpu.VMEM)
    smem = pl.BlockSpec(memory_space=pltpu.SMEM)
    dma = pltpu.SemaphoreType.DMA
    lanes = 2 * PADB
    return pl.pallas_call(
        rail_kernel,
        out_shape=(
            jax.ShapeDtypeStruct((DEPTH, CELLS_HERE), jnp.float32),
            jax.ShapeDtypeStruct((DEPTH, CELLS_HERE), jnp.bfloat16),
        ),
        in_specs=[vmem] * 3 + [smem] * 2 + [vmem] * 7,
        out_specs=(vmem, vmem),
        scratch_shapes=[
            pltpu.VMEM((PAD, CELLS_HERE), jnp.float32),
            pltpu.VMEM((2 * TALL + PAD, BROAD), jnp.float32),
            pltpu.VMEM((GROUP, 1, lanes), jnp.float32),
            pltpu.VMEM((GROUP, 1, lanes), jnp.float32),
            pltpu.VMEM((ZS, lanes), jnp.float32),
            pltpu.VMEM((PLACES, ZS, lanes), jnp.float32),
            pltpu.VMEM((ZS, 1, lanes), jnp.float32),
            pltpu.VMEM((GROUP, 1, lanes), jnp.float32),
            dma((18,)), dma, dma, dma, dma, dma, dma, dma,
        ],
        compiler_params=pltpu.CompilerParams(collective_id=0, has_side_effects=True),
    )(
        displacement, earlier_field, region_ids.reshape(1, CELLS_HERE), material, band_edges,
        mode_shapes.T, *[jnp.asarray(t) for t in TABLES],
    )


def solution(mesh):
    return jax.shard_map(
        body,
        mesh=mesh,
        in_specs=(P("slab", "sec"), P("slab", "sec"), P("sec"), P(), P("sec", None), P()),
        out_specs=(P("slab", "sec"), P("slab", "sec")),
        check_vma=False,
    )
```

```python
import functools
import math

import jax
import jax.numpy as jnp
import numpy as np
from jax import lax
from jax.experimental import pallas as pl
from jax.experimental.pallas import tpu as pltpu
from jax.sharding import PartitionSpec as P

COLS = 64
MODES = 64
WAVES = 4096
REGIONS = 8
STEPS = 4
PLANES = 5120
SLABS = 128
SECS = 4
DEPTH = PLANES // SLABS
PAD = 8
EDGE = STEPS * COLS
CELLS_HERE = 4096 // SECS
TALL = DEPTH + 2 * PAD
BROAD = CELLS_HERE + 2 * EDGE
BESIDE = ((0, 1), (0, -1), (1, 0), (-1, 0), (1, 1), (1, -1), (-1, 1), (-1, -1))
PADB = 64
K1 = WAVES // SLABS
ZS = 8
PLACES = SLABS // ZS
GROUP = ZS * SECS
MESH = pl.DeviceIdType.MESH

courant_sq = 0.14
two_pi = 2.0 * math.pi
HIGHEST = lax.Precision.HIGHEST


def make_tables():
    k2 = np.arange(SLABS)
    held_a = (np.arange(ZS)[None, :] * PLACES + np.arange(PLACES)[:, None]).reshape(-1)
    first = two_pi * (np.outer(k2, held_a) % SLABS) / SLABS
    dft_a = np.concatenate([np.cos(first), -np.sin(first)], axis=0)
    b = np.arange(PADB)
    live = (b < DEPTH).astype(np.float64)
    phi = two_pi * np.outer(k2, b) / PLANES
    tw_cos = np.tile(np.cos(phi) * live, (1, 2))
    tw_sin = np.tile(np.sin(phi) * live, (1, 2))
    psi = two_pi * (np.outer(b, np.arange(K1)) % DEPTH) / DEPTH
    pair = np.eye(2)
    c = np.kron(pair, np.cos(psi) * live[:, None])
    s = np.kron(pair, np.sin(psi) * live[:, None])
    forward = np.block([[c, -s], [s, c]])
    inverse = np.block([[c.T, s.T], [-s.T, c.T]])
    at = held_a.reshape(PLACES, ZS, 1) * k2
    last = two_pi * (at % SLABS) / SLABS
    rows = np.concatenate([np.cos(last), -np.sin(last)], axis=2) * (2.0 / PLANES)
    return [t.astype(np.float32) for t in (rows, dft_a, tw_cos, tw_sin, forward, inverse)]


TABLES = make_tables()


def rail_kernel(
    disp_ref, earlier_ref, region_ref, material_ref, edges_ref, shapes_hbm,
    rows_hbm, dft_hbm, twc_hbm, tws_hbm, fwd_hbm, inv_hbm,
    out_ref, band_ref,
    shapes_ref, rows_ref, dft_ref, twc_ref, tws_ref, fwd_ref, inv_ref, table_sem,
    blank_ref, stiff_ref, wide, modal_ref, pieces, mine, held, sent, smooth_ref,
    send0, recv0, send1, recv1, send2, recv2, send3, recv3,
):
    slab = lax.axis_index("slab")
    sec = lax.axis_index("sec")
    z, place = slab // PLACES, slab % PLACES
    group = z * SECS + sec

    def in_group(step):
        other = lax.rem(group + step, GROUP)
        other_z = other // SECS
        return other, other_z, {"slab": other_z * PLACES + place, "sec": lax.rem(other, SECS)}

    def in_places(step):
        return {"slab": z * PLACES + lax.rem(place + step, PLACES), "sec": sec}

    def beside(up, across):
        return {
            "slab": lax.rem(slab + (SLABS + up), SLABS),
            "sec": lax.rem(sec + (SECS + across), SECS),
        }

    barrier = pltpu.get_barrier_semaphore()

    tables = [
        pltpu.make_async_copy(src, dst, table_sem.at[i])
        for i, (src, dst) in enumerate(
            (
                (shapes_hbm, shapes_ref), (rows_hbm.at[place], rows_ref), (dft_hbm, dft_ref),
                (twc_hbm, twc_ref), (tws_hbm, tws_ref), (fwd_hbm, fwd_ref), (inv_hbm, inv_ref),
            )
        )
    ]

    @pl.loop(1, GROUP)
    def _(step):
        pl.semaphore_signal(barrier, inc=1, device_id=in_group(step)[2], device_id_type=MESH)

    @pl.loop(1, PLACES)
    def _(step):
        pl.semaphore_signal(barrier, inc=1, device_id=in_places(step), device_id_type=MESH)

    for up, across in BESIDE:
        pl.semaphore_signal(barrier, inc=1, device_id=beside(up, across), device_id_type=MESH)

    for table in tables:
        table.start()
    stiff = jnp.zeros((8, CELLS_HERE), jnp.float32)
    region = jnp.broadcast_to(region_ref[...], (8, CELLS_HERE))
    for r in range(REGIONS):
        value = courant_sq * material_ref[0, r] * material_ref[1, r]
        stiff = jnp.where(region == r, value, stiff)
    stiff_ref[...] = stiff
    blank_ref[...] = jnp.zeros((DEPTH, EDGE), jnp.float32)
    for at in (0, TALL - STEPS, TALL, 2 * TALL - STEPS):
        wide[at : at + STEPS, :] = jnp.zeros((STEPS, BROAD), jnp.float32)

    pl.semaphore_wait(barrier, GROUP + PLACES - 2 + len(BESIDE))

    halo_copies = []

    def send_halo(src, base, src_rows, dst_rows, up, across):
        src_at, dst_at = {-1: (0, EDGE + CELLS_HERE), 1: (CELLS_HERE - EDGE, 0), 0: (0, EDGE)}[across]
        count = CELLS_HERE if across == 0 else EDGE
        src = src.at[pl.ds(*src_rows), pl.ds(src_at, count)]
        dst = wide.at[pl.ds(base + dst_rows, src_rows[1]), pl.ds(dst_at, count)]
        if up == 0 and across == 0:
            pltpu.make_async_copy(src, dst, recv0).start()
            return
        copy = pltpu.make_async_remote_copy(
            src_ref=src, dst_ref=dst, send_sem=send0.at[len(halo_copies)], recv_sem=recv0,
            device_id=beside(up, across), device_id_type=MESH,
        )
        reach = {-1: sec > 0, 0: None, 1: sec < SECS - 1}[across]
        halo_copies.append((copy, reach))
        if across == 0:
            copy.start()
            return
        pl.when(reach)(copy.start)
        lacking = sec == 0 if across == 1 else sec == SECS - 1
        zeros = blank_ref.at[pl.ds(0, src_rows[1]), :]
        pl.when(lacking)(pltpu.make_async_copy(zeros, dst, recv0).start)

    for up, across in BESIDE + ((0, 0),):
        src_rows, dst_rows = {
            -1: ((0, STEPS), PAD + DEPTH),
            1: ((DEPTH - STEPS, STEPS), PAD - STEPS),
            0: ((0, DEPTH), PAD),
        }[up]
        send_halo(disp_ref, 0, src_rows, dst_rows, up, across)
        send_halo(earlier_ref, TALL, src_rows, dst_rows, up, across)
        if up == 0:
            send_halo(stiff_ref, 2 * TALL, (0, PAD), 0, up, across)
    for table in tables:
        table.wait()
    arrived = wide.at[pl.ds(0, 2 * (DEPTH + 2 * STEPS) + PAD), :]
    pltpu.make_async_copy(arrived, arrived, recv0).wait()

    lane = lax.broadcasted_iota(jnp.int32, (1, BROAD), 1)
    current = wide[:TALL, :]
    before = wide[TALL : 2 * TALL, :]
    stiff = wide[2 * TALL : 2 * TALL + 1, :]
    not_first = lane % COLS > 0
    not_last = lane % COLS < COLS - 1
    for _ in range(STEPS):
        west = jnp.where(not_first, pltpu.roll(current, 1, 1), 0.0)
        east = jnp.where(not_last, pltpu.roll(current, BROAD - 1, 1), 0.0)
        above = pltpu.roll(current, COLS, 1)
        below = pltpu.roll(current, BROAD - COLS, 1)
        prior = pltpu.roll(current, 1, 0)
        later = pltpu.roll(current, TALL - 1, 0)
        summed = prior + later + above + below + west + east
        current, before = (
            2.0 * current - before + stiff * (summed - 6.0 * current),
            current,
        )
    final = current[PAD : PAD + DEPTH, EDGE : EDGE + CELLS_HERE]
    out_ref[...] = final
    lanes = 2 * PADB
    shapes = shapes_ref[...]
    padded = jnp.concatenate([final, jnp.zeros((lanes - DEPTH, CELLS_HERE), jnp.float32)], axis=0)
    modal = lax.dot_general(
        shapes, padded, (((1,), (1,)), ((), ())),
        precision=HIGHEST, preferred_element_type=jnp.float32,
    )
    modal = modal[:GROUP] + pltpu.roll(modal[GROUP:], PADB, 1)
    for i in range(GROUP):
        modal_ref[i] = modal[i : i + 1, :]

    @pl.loop(1, GROUP)
    def _(step):
        other, _, device = in_group(step)
        pltpu.make_async_remote_copy(
            src_ref=modal_ref.at[other], dst_ref=pieces.at[group],
            send_sem=send1, recv_sem=recv1, device_id=device, device_id_type=MESH,
        ).start()

    pltpu.make_async_copy(modal_ref.at[group], pieces.at[group], recv1).start()
    pltpu.make_async_copy(pieces, pieces, recv1).wait()
    for i in range(ZS):
        total = pieces[SECS * i] + pieces[SECS * i + 1]
        total = total + pieces[SECS * i + 2] + pieces[SECS * i + 3]
        mine[i : i + 1, :] = total

    @pl.loop(1, PLACES)
    def _(step):
        pltpu.make_async_remote_copy(
            src_ref=mine, dst_ref=held.at[place],
            send_sem=send2, recv_sem=recv2, device_id=in_places(step), device_id_type=MESH,
        ).start()

    pltpu.make_async_copy(mine, held.at[place], recv2).start()
    pltpu.make_async_copy(held, held, recv2).wait()

    dot = functools.partial(jnp.dot, precision=HIGHEST, preferred_element_type=jnp.float32)
    twc = twc_ref[...]
    tws = tws_ref[...]
    row = lax.broadcasted_iota(jnp.int32, (SLABS, 4 * K1), 0)
    lane = lax.broadcasted_iota(jnp.int32, (SLABS, 4 * K1), 1)
    wave = row + SLABS * (lane % K1)
    is_front = lane % (2 * K1) < K1
    lower = jnp.where(is_front, edges_ref[0, group], edges_ref[0, group + GROUP])
    upper = jnp.where(is_front, edges_ref[1, group], edges_ref[1, group + GROUP])
    both = dot(dft_ref[...], held[...].reshape(SLABS, lanes))
    real, imag = both[:SLABS], both[SLABS:]
    twisted = jnp.concatenate([real * twc + imag * tws, imag * twc - real * tws], axis=1)
    spectrum = dot(twisted, fwd_ref[...])
    in_band = (wave >= lower) & (wave < upper)
    filtered = jnp.where(in_band, spectrum, 0.0)
    back = dot(filtered, inv_ref[...])
    real, imag = back[:, :lanes], back[:, lanes:]
    twisted = jnp.concatenate([real * twc - imag * tws, imag * twc + real * tws], axis=0)
    smooth = dot(rows_ref[...], twisted)
    for i in range(ZS):
        sent[i] = smooth[i : i + 1, :]

    @pl.loop(1, GROUP)
    def _(step):
        _, other_z, device = in_group(step)
        pltpu.make_async_remote_copy(
            src_ref=sent.at[other_z], dst_ref=smooth_ref.at[group],
            send_sem=send3, recv_sem=recv3, device_id=device, device_id_type=MESH,
        ).start()

    pltpu.make_async_copy(sent.at[z], smooth_ref.at[group], recv3).start()
    pltpu.make_async_copy(smooth_ref, smooth_ref, recv3).wait()
    gathered = smooth_ref[:, 0, :]
    gathered = jnp.concatenate([gathered, pltpu.roll(gathered, PADB, 1)], axis=0).T
    band = dot(gathered[:DEPTH], shapes)
    band_ref[...] = band.astype(jnp.bfloat16)
    for copy, reach in halo_copies:
        if reach is None:
            copy.wait_send()
        else:
            pl.when(reach)(copy.wait_send)
    most = pieces.at[pl.ds(0, GROUP - 1)]
    pltpu.make_async_copy(most, most, send1).wait()
    most = held.at[pl.ds(0, PLACES - 1)]
    pltpu.make_async_copy(most, most, send2).wait()
    most = smooth_ref.at[pl.ds(0, GROUP - 1)]
    pltpu.make_async_copy(most, most, send3).wait()


def body(displacement, earlier_field, region_ids, material, mode_shapes, band_edges):
    vmem = pl.BlockSpec(memory_space=pltpu.VMEM)
    smem = pl.BlockSpec(memory_space=pltpu.SMEM)
    dma = pltpu.SemaphoreType.DMA
    lanes = 2 * PADB
    return pl.pallas_call(
        rail_kernel,
        out_shape=(
            jax.ShapeDtypeStruct((DEPTH, CELLS_HERE), jnp.float32),
            jax.ShapeDtypeStruct((DEPTH, CELLS_HERE), jnp.bfloat16),
        ),
        in_specs=[vmem] * 3 + [smem] * 2 + [pl.BlockSpec(memory_space=pl.ANY)] * 7,
        out_specs=(vmem, vmem),
        scratch_shapes=[
            pltpu.VMEM((MODES, CELLS_HERE), jnp.float32),
            pltpu.VMEM(TABLES[0].shape[1:], jnp.float32),
            *[pltpu.VMEM(t.shape, jnp.float32) for t in TABLES[1:]],
            dma((7,)),
            pltpu.VMEM((DEPTH, EDGE), jnp.float32),
            pltpu.VMEM((PAD, CELLS_HERE), jnp.float32),
            pltpu.VMEM((2 * TALL + PAD, BROAD), jnp.float32),
            pltpu.VMEM((GROUP, 1, lanes), jnp.float32),
            pltpu.VMEM((GROUP, 1, lanes), jnp.float32),
            pltpu.VMEM((ZS, lanes), jnp.float32),
            pltpu.VMEM((PLACES, ZS, lanes), jnp.float32),
            pltpu.VMEM((ZS, 1, lanes), jnp.float32),
            pltpu.VMEM((GROUP, 1, lanes), jnp.float32),
            dma((18,)), dma, dma, dma, dma, dma, dma, dma,
        ],
        compiler_params=pltpu.CompilerParams(collective_id=0, has_side_effects=True),
    )(
        displacement, earlier_field, region_ids.reshape(1, CELLS_HERE), material, band_edges,
        mode_shapes.T, *[jnp.asarray(t) for t in TABLES],
    )


def solution(mesh):
    return jax.shard_map(
        body,
        mesh=mesh,
        in_specs=(P("slab", "sec"), P("slab", "sec"), P("sec"), P(), P("sec", None), P()),
        out_specs=(P("slab", "sec"), P("slab", "sec")),
        check_vma=False,
    )
```

```python
import functools
import math

import jax
import jax.numpy as jnp
import numpy as np
from jax import lax
from jax.experimental import pallas as pl
from jax.experimental.pallas import tpu as pltpu
from jax.sharding import PartitionSpec as P

COLS = 64
MODES = 64
WAVES = 4096
REGIONS = 8
STEPS = 4
PLANES = 5120
SLABS = 128
SECS = 4
DEPTH = PLANES // SLABS
PAD = 8
EDGE = STEPS * COLS
CELLS_HERE = 4096 // SECS
TALL = DEPTH + 2 * PAD
BROAD = CELLS_HERE + 2 * EDGE
BESIDE = ((0, 1), (0, -1), (1, 0), (-1, 0), (1, 1), (1, -1), (-1, 1), (-1, -1))
PADB = 64
K1 = WAVES // SLABS
ZS = 8
PLACES = SLABS // ZS
GROUP = ZS * SECS
MESH = pl.DeviceIdType.MESH

courant_sq = 0.14
two_pi = 2.0 * math.pi


def make_tables():
    k2 = np.arange(SLABS)
    held_a = (np.arange(ZS)[None, :] * PLACES + np.arange(PLACES)[:, None]).reshape(-1)
    first = two_pi * (np.outer(k2, held_a) % SLABS) / SLABS
    dft_a = np.concatenate([np.cos(first), -np.sin(first)], axis=0)
    b = np.arange(PADB)
    live = (b < DEPTH).astype(np.float64)
    phi = two_pi * np.outer(k2, b) / PLANES
    tw_cos = np.tile(np.cos(phi) * live, (1, 2))
    tw_sin = np.tile(np.sin(phi) * live, (1, 2))
    psi = two_pi * (np.outer(b, np.arange(K1)) % DEPTH) / DEPTH
    pair = np.eye(2)
    c = np.kron(pair, np.cos(psi) * live[:, None])
    s = np.kron(pair, np.sin(psi) * live[:, None])
    forward = np.block([[c, -s], [s, c]])
    inverse = np.block([[c.T, s.T], [-s.T, c.T]])
    at = held_a.reshape(PLACES, ZS, 1) * k2
    last = two_pi * (at % SLABS) / SLABS
    rows = np.concatenate([np.cos(last), -np.sin(last)], axis=2) * (2.0 / PLANES)
    return [t.astype(np.float32) for t in (rows, dft_a, tw_cos, tw_sin, forward, inverse)]


TABLES = make_tables()


def far_first(turn, count):
    return count // 2 + (turn + 1) // 2 * (1 - 2 * (turn % 2))


def split(x):
    high = x.astype(jnp.bfloat16)
    return high, (x - high.astype(jnp.float32)).astype(jnp.bfloat16)


def dot3(x, y, dims=(((1,), (0,)), ((), ()))):
    (xh, xl), (yh, yl) = split(x), split(y)
    one = functools.partial(
        lax.dot_general, dimension_numbers=dims, preferred_element_type=jnp.float32
    )
    return one(xh, yh) + (one(xh, yl) + one(xl, yh))


def finish_kernel(final_ref, smooth_ref, shapes_ref, out_ref, band_ref):
    out_ref[...] = final_ref[...]
    gathered = smooth_ref[:, 0, :]
    gathered = jnp.concatenate([gathered, pltpu.roll(gathered, PADB, 1)], axis=0).T
    band_ref[...] = dot3(gathered[:DEPTH], shapes_ref[...]).astype(jnp.bfloat16)


def rail_kernel(
    disp_ref, earlier_ref, region_ref, material_ref, edges_ref, shapes_hbm,
    rows_hbm, dft_hbm, twc_hbm, tws_hbm, fwd_hbm, inv_hbm,
    out_ref, smooth_ref,
    shapes_ref, rows_ref, dft_ref, twc_ref, tws_ref, fwd_ref, inv_ref, table_sem,
    blank_ref, stiff_ref, wide, modal_ref, pieces, mine, held, sent,
    send0, recv0, send1, recv1, send2, recv2, send3, recv3,
):
    slab = lax.axis_index("slab")
    sec = lax.axis_index("sec")
    z, place = slab // PLACES, slab % PLACES
    group = z * SECS + sec

    def in_group(step):
        other = lax.rem(group + step, GROUP)
        other_z = other // SECS
        return other, other_z, {"slab": other_z * PLACES + place, "sec": lax.rem(other, SECS)}

    def in_places(step):
        return {"slab": z * PLACES + lax.rem(place + step, PLACES), "sec": sec}

    def beside(up, across):
        return {
            "slab": lax.rem(slab + (SLABS + up), SLABS),
            "sec": lax.rem(sec + (SECS + across), SECS),
        }

    barrier = pltpu.get_barrier_semaphore()

    tables = [
        pltpu.make_async_copy(src, dst, table_sem.at[i])
        for i, (src, dst) in enumerate(
            (
                (shapes_hbm, shapes_ref), (rows_hbm.at[place], rows_ref), (dft_hbm, dft_ref),
                (twc_hbm, twc_ref), (tws_hbm, tws_ref), (fwd_hbm, fwd_ref), (inv_hbm, inv_ref),
            )
        )
    ]

    @pl.loop(0, GROUP - 1)
    def _(turn):
        step = far_first(turn, GROUP)
        pl.semaphore_signal(barrier, inc=1, device_id=in_group(step)[2], device_id_type=MESH)

    @pl.loop(0, PLACES - 1)
    def _(turn):
        step = far_first(turn, PLACES)
        pl.semaphore_signal(barrier, inc=1, device_id=in_places(step), device_id_type=MESH)

    for up, across in BESIDE:
        pl.semaphore_signal(barrier, inc=1, device_id=beside(up, across), device_id_type=MESH)

    for table in tables:
        table.start()
    stiff = jnp.zeros((8, CELLS_HERE), jnp.float32)
    region = jnp.broadcast_to(region_ref[...], (8, CELLS_HERE))
    for r in range(REGIONS):
        value = courant_sq * material_ref[0, r] * material_ref[1, r]
        stiff = jnp.where(region == r, value, stiff)
    stiff_ref[...] = stiff
    blank_ref[...] = jnp.zeros((DEPTH, EDGE), jnp.float32)
    for at in (0, TALL - STEPS, TALL, 2 * TALL - STEPS):
        wide[at : at + STEPS, :] = jnp.zeros((STEPS, BROAD), jnp.float32)

    pl.semaphore_wait(barrier, GROUP + PLACES - 2 + len(BESIDE))

    halo_copies = []

    def send_halo(src, base, src_rows, dst_rows, up, across):
        src_at, dst_at = {-1: (0, EDGE + CELLS_HERE), 1: (CELLS_HERE - EDGE, 0), 0: (0, EDGE)}[across]
        count = CELLS_HERE if across == 0 else EDGE
        src = src.at[pl.ds(*src_rows), pl.ds(src_at, count)]
        dst = wide.at[pl.ds(base + dst_rows, src_rows[1]), pl.ds(dst_at, count)]
        if up == 0 and across == 0:
            pltpu.make_async_copy(src, dst, recv0).start()
            return
        copy = pltpu.make_async_remote_copy(
            src_ref=src, dst_ref=dst, send_sem=send0.at[len(halo_copies)], recv_sem=recv0,
            device_id=beside(up, across), device_id_type=MESH,
        )
        reach = {-1: sec > 0, 0: None, 1: sec < SECS - 1}[across]
        halo_copies.append((copy, reach))
        if across == 0:
            copy.start()
            return
        pl.when(reach)(copy.start)
        lacking = sec == 0 if across == 1 else sec == SECS - 1
        zeros = blank_ref.at[pl.ds(0, src_rows[1]), :]
        pl.when(lacking)(pltpu.make_async_copy(zeros, dst, recv0).start)

    for up, across in BESIDE + ((0, 0),):
        src_rows, dst_rows = {
            -1: ((0, STEPS), PAD + DEPTH),
            1: ((DEPTH - STEPS, STEPS), PAD - STEPS),
            0: ((0, DEPTH), PAD),
        }[up]
        send_halo(disp_ref, 0, src_rows, dst_rows, up, across)
        send_halo(earlier_ref, TALL, src_rows, dst_rows, up, across)
        if up == 0:
            send_halo(stiff_ref, 2 * TALL, (0, PAD), 0, up, across)
    for table in tables:
        table.wait()
    arrived = wide.at[pl.ds(0, 2 * (DEPTH + 2 * STEPS) + PAD), :]
    pltpu.make_async_copy(arrived, arrived, recv0).wait()

    lane = lax.broadcasted_iota(jnp.int32, (1, BROAD), 1)
    current = wide[:TALL, :]
    before = wide[TALL : 2 * TALL, :]
    stiff = wide[2 * TALL : 2 * TALL + 1, :]
    not_first = lane % COLS > 0
    not_last = lane % COLS < COLS - 1
    for _ in range(STEPS):
        west = jnp.where(not_first, pltpu.roll(current, 1, 1), 0.0)
        east = jnp.where(not_last, pltpu.roll(current, BROAD - 1, 1), 0.0)
        above = pltpu.roll(current, COLS, 1)
        below = pltpu.roll(current, BROAD - COLS, 1)
        prior = pltpu.roll(current, 1, 0)
        later = pltpu.roll(current, TALL - 1, 0)
        summed = prior + later + above + below + west + east
        current, before = (
            2.0 * current - before + stiff * (summed - 6.0 * current),
            current,
        )
    final = current[PAD : PAD + DEPTH, EDGE : EDGE + CELLS_HERE]
    out_ref[...] = final
    lanes = 2 * PADB
    shapes = shapes_ref[...]
    padded = jnp.concatenate([final, jnp.zeros((lanes - DEPTH, CELLS_HERE), jnp.float32)], axis=0)
    modal = dot3(shapes, padded, (((1,), (1,)), ((), ())))
    modal = modal[:GROUP] + pltpu.roll(modal[GROUP:], PADB, 1)
    for i in range(GROUP):
        modal_ref[i] = modal[i : i + 1, :]

    @pl.loop(0, GROUP - 1)
    def _(turn):
        step = far_first(turn, GROUP)
        other, _, device = in_group(step)
        pltpu.make_async_remote_copy(
            src_ref=modal_ref.at[other], dst_ref=pieces.at[group],
            send_sem=send1, recv_sem=recv1, device_id=device, device_id_type=MESH,
        ).start()

    pltpu.make_async_copy(modal_ref.at[group], pieces.at[group], recv1).start()
    pltpu.make_async_copy(pieces, pieces, recv1).wait()
    for i in range(ZS):
        total = pieces[SECS * i] + pieces[SECS * i + 1]
        total = total + pieces[SECS * i + 2] + pieces[SECS * i + 3]
        mine[i : i + 1, :] = total

    @pl.loop(0, PLACES - 1)
    def _(turn):
        step = far_first(turn, PLACES)
        pltpu.make_async_remote_copy(
            src_ref=mine, dst_ref=held.at[place],
            send_sem=send2, recv_sem=recv2, device_id=in_places(step), device_id_type=MESH,
        ).start()

    pltpu.make_async_copy(mine, held.at[place], recv2).start()
    pltpu.make_async_copy(held, held, recv2).wait()

    twc = twc_ref[...]
    tws = tws_ref[...]
    row = lax.broadcasted_iota(jnp.int32, (SLABS, 4 * K1), 0)
    lane = lax.broadcasted_iota(jnp.int32, (SLABS, 4 * K1), 1)
    wave = row + SLABS * (lane % K1)
    is_front = lane % (2 * K1) < K1
    lower = jnp.where(is_front, edges_ref[0, group], edges_ref[0, group + GROUP])
    upper = jnp.where(is_front, edges_ref[1, group], edges_ref[1, group + GROUP])
    both = dot3(dft_ref[...], held[...].reshape(SLABS, lanes))
    real, imag = both[:SLABS], both[SLABS:]
    twisted = jnp.concatenate([real * twc + imag * tws, imag * twc - real * tws], axis=1)
    spectrum = dot3(twisted, fwd_ref[...])
    in_band = (wave >= lower) & (wave < upper)
    filtered = jnp.where(in_band, spectrum, 0.0)
    back = dot3(filtered, inv_ref[...])
    real, imag = back[:, :lanes], back[:, lanes:]
    twisted = jnp.concatenate([real * twc - imag * tws, imag * twc + real * tws], axis=0)
    smooth = dot3(rows_ref[...], twisted)
    for i in range(ZS):
        sent[i] = smooth[i : i + 1, :]

    @pl.loop(0, GROUP - 1)
    def _(turn):
        step = far_first(turn, GROUP)
        _, other_z, device = in_group(step)
        pltpu.make_async_remote_copy(
            src_ref=sent.at[other_z], dst_ref=smooth_ref.at[group],
            send_sem=send3, recv_sem=recv3, device_id=device, device_id_type=MESH,
        ).start()

    pltpu.make_async_copy(sent.at[z], smooth_ref.at[group], recv3).start()
    pltpu.make_async_copy(smooth_ref, smooth_ref, recv3).wait()
    for copy, reach in halo_copies:
        if reach is None:
            copy.wait_send()
        else:
            pl.when(reach)(copy.wait_send)
    most = pieces.at[pl.ds(0, GROUP - 1)]
    pltpu.make_async_copy(most, most, send1).wait()
    most = held.at[pl.ds(0, PLACES - 1)]
    pltpu.make_async_copy(most, most, send2).wait()
    most = smooth_ref.at[pl.ds(0, GROUP - 1)]
    pltpu.make_async_copy(most, most, send3).wait()


def body(displacement, earlier_field, region_ids, material, mode_shapes, band_edges):
    vmem = pl.BlockSpec(memory_space=pltpu.VMEM)
    smem = pl.BlockSpec(memory_space=pltpu.SMEM)
    dma = pltpu.SemaphoreType.DMA
    lanes = 2 * PADB
    shapes = mode_shapes.T
    final, smooth = pl.pallas_call(
        rail_kernel,
        out_shape=(
            jax.ShapeDtypeStruct((DEPTH, CELLS_HERE), jnp.float32),
            jax.ShapeDtypeStruct((GROUP, 1, lanes), jnp.float32),
        ),
        in_specs=[vmem] * 3 + [smem] * 2 + [pl.BlockSpec(memory_space=pl.ANY)] * 7,
        out_specs=(vmem, vmem),
        scratch_shapes=[
            pltpu.VMEM((MODES, CELLS_HERE), jnp.float32),
            pltpu.VMEM(TABLES[0].shape[1:], jnp.float32),
            *[pltpu.VMEM(t.shape, jnp.float32) for t in TABLES[1:]],
            dma((7,)),
            pltpu.VMEM((DEPTH, EDGE), jnp.float32),
            pltpu.VMEM((PAD, CELLS_HERE), jnp.float32),
            pltpu.VMEM((2 * TALL + PAD, BROAD), jnp.float32),
            pltpu.VMEM((GROUP, 1, lanes), jnp.float32),
            pltpu.VMEM((GROUP, 1, lanes), jnp.float32),
            pltpu.VMEM((ZS, lanes), jnp.float32),
            pltpu.VMEM((PLACES, ZS, lanes), jnp.float32),
            pltpu.VMEM((ZS, 1, lanes), jnp.float32),
            dma((18,)), dma, dma, dma, dma, dma, dma, dma,
        ],
        compiler_params=pltpu.CompilerParams(collective_id=0, has_side_effects=True),
    )(
        displacement, earlier_field, region_ids.reshape(1, CELLS_HERE), material, band_edges,
        shapes, *[jnp.asarray(t) for t in TABLES],
    )
    return pl.pallas_call(
        finish_kernel,
        out_shape=(
            jax.ShapeDtypeStruct((DEPTH, CELLS_HERE), jnp.float32),
            jax.ShapeDtypeStruct((DEPTH, CELLS_HERE), jnp.bfloat16),
        ),
    )(final, smooth, shapes)


def solution(mesh):
    return jax.shard_map(
        body,
        mesh=mesh,
        in_specs=(P("slab", "sec"), P("slab", "sec"), P("sec"), P(), P("sec", None), P()),
        out_specs=(P("slab", "sec"), P("slab", "sec")),
        check_vma=False,
    )
```

```python
import functools
import math

import jax
import jax.numpy as jnp
import numpy as np
from jax import lax
from jax.experimental import pallas as pl
from jax.experimental.pallas import tpu as pltpu
from jax.sharding import PartitionSpec as P

COLS = 64
MODES = 64
WAVES = 4096
REGIONS = 8
STEPS = 4
PLANES = 5120
SLABS = 128
SECS = 4
DEPTH = PLANES // SLABS
PAD = 8
EDGE = STEPS * COLS
CELLS_HERE = 4096 // SECS
TALL = DEPTH + 2 * PAD
BROAD = CELLS_HERE + 2 * EDGE
BESIDE = ((0, 1), (0, -1), (1, 0), (-1, 0), (1, 1), (1, -1), (-1, 1), (-1, -1))
PADB = 64
K1 = WAVES // SLABS
YS = 4
PLACES = SLABS // YS
GROUP = YS * SECS
TILES = 2
MESH = pl.DeviceIdType.MESH

courant_sq = 0.14
two_pi = 2.0 * math.pi


def make_tables():
    k2 = np.arange(SLABS)
    held_a = np.arange(SLABS).reshape(PLACES, 1, YS) + np.zeros((1, TILES, 1), np.int64)
    first = two_pi * (np.outer(k2, held_a.reshape(-1)) % SLABS) / SLABS
    held_t = np.broadcast_to(np.arange(TILES)[None, :, None], held_a.shape).reshape(1, -1)
    own = [held_t == t for t in range(TILES)]
    dft_a = np.concatenate(
        [np.cos(first) * m for m in own] + [-np.sin(first) * m for m in own], axis=0
    )
    b = np.arange(PADB)
    live = (b < DEPTH).astype(np.float64)
    phi = two_pi * np.outer(k2, b) / PLANES
    tw_cos = np.tile(np.cos(phi) * live, (1, 2))
    tw_sin = np.tile(np.sin(phi) * live, (1, 2))
    psi = two_pi * (np.outer(b, np.arange(K1)) % DEPTH) / DEPTH
    pair = np.eye(2)
    c = np.kron(pair, np.cos(psi) * live[:, None])
    s = np.kron(pair, np.sin(psi) * live[:, None])
    forward = np.block([[c, -s], [s, c]])
    inverse = np.block([[c.T, s.T], [-s.T, c.T]])
    last = two_pi * (np.arange(SLABS).reshape(PLACES, YS, 1) * k2 % SLABS) / SLABS
    rows = np.zeros((PLACES, TILES, YS, 2, TILES, SLABS))
    for t in range(TILES):
        rows[:, t, :, 0, t] = np.cos(last)
        rows[:, t, :, 1, t] = -np.sin(last)
    rows = rows.reshape(PLACES, TILES * YS, 2 * TILES * SLABS) * (2.0 / PLANES)
    return [t.astype(np.float32) for t in (rows, dft_a, tw_cos, tw_sin, forward, inverse)]


TABLES = make_tables()


def far_first(turn, count):
    return count // 2 + (turn + 1) // 2 * (1 - 2 * (turn % 2))


def split(x):
    high = x.astype(jnp.bfloat16)
    return high, (x - high.astype(jnp.float32)).astype(jnp.bfloat16)


def dot3(x, y, dims=(((1,), (0,)), ((), ()))):
    (xh, xl), (yh, yl) = split(x), split(y)
    one = functools.partial(
        lax.dot_general, dimension_numbers=dims, preferred_element_type=jnp.float32
    )
    return one(xh, yh) + (one(xh, yl) + one(xl, yh))


def finish_kernel(final_ref, smooth_ref, shapes_ref, out_ref, band_ref):
    out_ref[...] = final_ref[...]
    gathered = jnp.concatenate([smooth_ref[:, t, :] for t in range(TILES)], axis=0)
    gathered = jnp.concatenate([gathered, pltpu.roll(gathered, PADB, 1)], axis=0).T
    band_ref[...] = dot3(gathered[:DEPTH], shapes_ref[...]).astype(jnp.bfloat16)


def rail_kernel(
    disp_ref, earlier_ref, region_ref, material_ref, edges_ref, shapes_hbm,
    rows_hbm, dft_hbm, twc_hbm, tws_hbm, fwd_hbm, inv_hbm,
    out_ref, smooth_ref,
    shapes_ref, rows_ref, dft_ref, twc_ref, tws_ref, fwd_ref, inv_ref, table_sem,
    blank_ref, stiff_ref, wide, modal_ref, pieces, mine, held, sent,
    send0, recv0, send1, recv1, send2, recv2, send3, recv3,
):
    slab = lax.axis_index("slab")
    sec = lax.axis_index("sec")
    place, y = slab // YS, slab % YS
    group = y * SECS + sec

    def in_group(step):
        other = lax.rem(group + step, GROUP)
        other_y = other // SECS
        return other, other_y, {"slab": place * YS + other_y, "sec": lax.rem(other, SECS)}

    def in_places(step):
        return {"slab": lax.rem(place + step, PLACES) * YS + y, "sec": sec}

    def beside(up, across):
        return {
            "slab": lax.rem(slab + (SLABS + up), SLABS),
            "sec": lax.rem(sec + (SECS + across), SECS),
        }

    barrier = pltpu.get_barrier_semaphore()

    tables = [
        pltpu.make_async_copy(src, dst, table_sem.at[i])
        for i, (src, dst) in enumerate(
            (
                (shapes_hbm, shapes_ref), (rows_hbm.at[place], rows_ref), (dft_hbm, dft_ref),
                (twc_hbm, twc_ref), (tws_hbm, tws_ref), (fwd_hbm, fwd_ref), (inv_hbm, inv_ref),
            )
        )
    ]

    @pl.loop(0, GROUP - 1)
    def _(turn):
        step = far_first(turn, GROUP)
        pl.semaphore_signal(barrier, inc=1, device_id=in_group(step)[2], device_id_type=MESH)

    @pl.loop(0, PLACES - 1)
    def _(turn):
        step = far_first(turn, PLACES)
        pl.semaphore_signal(barrier, inc=1, device_id=in_places(step), device_id_type=MESH)

    for up, across in BESIDE:
        pl.semaphore_signal(barrier, inc=1, device_id=beside(up, across), device_id_type=MESH)

    for table in tables:
        table.start()
    stiff = jnp.zeros((8, CELLS_HERE), jnp.float32)
    region = jnp.broadcast_to(region_ref[...], (8, CELLS_HERE))
    for r in range(REGIONS):
        value = courant_sq * material_ref[0, r] * material_ref[1, r]
        stiff = jnp.where(region == r, value, stiff)
    stiff_ref[...] = stiff
    blank_ref[...] = jnp.zeros((DEPTH, EDGE), jnp.float32)
    for at in (0, TALL - STEPS, TALL, 2 * TALL - STEPS):
        wide[at : at + STEPS, :] = jnp.zeros((STEPS, BROAD), jnp.float32)

    pl.semaphore_wait(barrier, GROUP + PLACES - 2 + len(BESIDE))

    halo_copies = []

    def send_halo(src, base, src_rows, dst_rows, up, across):
        src_at, dst_at = {-1: (0, EDGE + CELLS_HERE), 1: (CELLS_HERE - EDGE, 0), 0: (0, EDGE)}[across]
        count = CELLS_HERE if across == 0 else EDGE
        src = src.at[pl.ds(*src_rows), pl.ds(src_at, count)]
        dst = wide.at[pl.ds(base + dst_rows, src_rows[1]), pl.ds(dst_at, count)]
        if up == 0 and across == 0:
            pltpu.make_async_copy(src, dst, recv0).start()
            return
        copy = pltpu.make_async_remote_copy(
            src_ref=src, dst_ref=dst, send_sem=send0.at[len(halo_copies)], recv_sem=recv0,
            device_id=beside(up, across), device_id_type=MESH,
        )
        reach = {-1: sec > 0, 0: None, 1: sec < SECS - 1}[across]
        halo_copies.append((copy, reach))
        if across == 0:
            copy.start()
            return
        pl.when(reach)(copy.start)
        lacking = sec == 0 if across == 1 else sec == SECS - 1
        zeros = blank_ref.at[pl.ds(0, src_rows[1]), :]
        pl.when(lacking)(pltpu.make_async_copy(zeros, dst, recv0).start)

    for up, across in BESIDE + ((0, 0),):
        src_rows, dst_rows = {
            -1: ((0, STEPS), PAD + DEPTH),
            1: ((DEPTH - STEPS, STEPS), PAD - STEPS),
            0: ((0, DEPTH), PAD),
        }[up]
        send_halo(disp_ref, 0, src_rows, dst_rows, up, across)
        send_halo(earlier_ref, TALL, src_rows, dst_rows, up, across)
        if up == 0:
            send_halo(stiff_ref, 2 * TALL, (0, PAD), 0, up, across)
    for table in tables:
        table.wait()
    arrived = wide.at[pl.ds(0, 2 * (DEPTH + 2 * STEPS) + PAD), :]
    pltpu.make_async_copy(arrived, arrived, recv0).wait()

    lane = lax.broadcasted_iota(jnp.int32, (1, BROAD), 1)
    current = wide[:TALL, :]
    before = wide[TALL : 2 * TALL, :]
    stiff = wide[2 * TALL : 2 * TALL + 1, :]
    not_first = lane % COLS > 0
    not_last = lane % COLS < COLS - 1
    for _ in range(STEPS):
        west = jnp.where(not_first, pltpu.roll(current, 1, 1), 0.0)
        east = jnp.where(not_last, pltpu.roll(current, BROAD - 1, 1), 0.0)
        above = pltpu.roll(current, COLS, 1)
        below = pltpu.roll(current, BROAD - COLS, 1)
        prior = pltpu.roll(current, 1, 0)
        later = pltpu.roll(current, TALL - 1, 0)
        summed = prior + later + above + below + west + east
        current, before = (
            2.0 * current - before + stiff * (summed - 6.0 * current),
            current,
        )
    final = current[PAD : PAD + DEPTH, EDGE : EDGE + CELLS_HERE]
    out_ref[...] = final
    lanes = 2 * PADB
    shapes = shapes_ref[...]
    padded = jnp.concatenate([final, jnp.zeros((lanes - DEPTH, CELLS_HERE), jnp.float32)], axis=0)
    modal = dot3(shapes, padded, (((1,), (1,)), ((), ())))
    modal = modal[: MODES // 2] + pltpu.roll(modal[MODES // 2 :], PADB, 1)
    for i in range(GROUP):
        for t in range(TILES):
            modal_ref[i, t : t + 1, :] = modal[i + GROUP * t : i + GROUP * t + 1, :]

    @pl.loop(0, GROUP - 1)
    def _(turn):
        step = far_first(turn, GROUP)
        other, _, device = in_group(step)
        pltpu.make_async_remote_copy(
            src_ref=modal_ref.at[other], dst_ref=pieces.at[group],
            send_sem=send1, recv_sem=recv1, device_id=device, device_id_type=MESH,
        ).start()

    pltpu.make_async_copy(modal_ref.at[group], pieces.at[group], recv1).start()
    pltpu.make_async_copy(pieces, pieces, recv1).wait()
    for i in range(YS):
        total = pieces[SECS * i] + pieces[SECS * i + 1]
        total = total + pieces[SECS * i + 2] + pieces[SECS * i + 3]
        for t in range(TILES):
            mine[YS * t + i : YS * t + i + 1, :] = total[t : t + 1, :]

    @pl.loop(0, PLACES - 1)
    def _(turn):
        step = far_first(turn, PLACES)
        pltpu.make_async_remote_copy(
            src_ref=mine, dst_ref=held.at[place],
            send_sem=send2, recv_sem=recv2, device_id=in_places(step), device_id_type=MESH,
        ).start()

    pltpu.make_async_copy(mine, held.at[place], recv2).start()
    pltpu.make_async_copy(held, held, recv2).wait()

    twc = jnp.concatenate([twc_ref[...]] * TILES, axis=0)
    tws = jnp.concatenate([tws_ref[...]] * TILES, axis=0)
    deep = TILES * SLABS
    row = lax.broadcasted_iota(jnp.int32, (deep, 4 * K1), 0)
    lane = lax.broadcasted_iota(jnp.int32, (deep, 4 * K1), 1)
    wave = row % SLABS + SLABS * (lane % K1)
    is_front = lane % (2 * K1) < K1

    def edge_of(side):
        values = []
        for t in range(TILES):
            mode = group + GROUP * t
            values.append(
                jnp.where(is_front, edges_ref[side, mode], edges_ref[side, mode + MODES // 2])
            )
        return jnp.where(row < SLABS, values[0], values[1])

    both = dot3(dft_ref[...], held[...].reshape(deep, lanes))
    real, imag = both[:deep], both[deep:]
    twisted = jnp.concatenate([real * twc + imag * tws, imag * twc - real * tws], axis=1)
    spectrum = dot3(twisted, fwd_ref[...])
    in_band = (wave >= edge_of(0)) & (wave < edge_of(1))
    filtered = jnp.where(in_band, spectrum, 0.0)
    back = dot3(filtered, inv_ref[...])
    real, imag = back[:, :lanes], back[:, lanes:]
    twisted = jnp.concatenate([real * twc - imag * tws, imag * twc + real * tws], axis=0)
    smooth = dot3(rows_ref[...], twisted)
    for i in range(YS):
        for t in range(TILES):
            sent[i, t : t + 1, :] = smooth[YS * t + i : YS * t + i + 1, :]

    @pl.loop(0, GROUP - 1)
    def _(turn):
        step = far_first(turn, GROUP)
        _, other_y, device = in_group(step)
        pltpu.make_async_remote_copy(
            src_ref=sent.at[other_y], dst_ref=smooth_ref.at[group],
            send_sem=send3, recv_sem=recv3, device_id=device, device_id_type=MESH,
        ).start()

    pltpu.make_async_copy(sent.at[y], smooth_ref.at[group], recv3).start()
    pltpu.make_async_copy(smooth_ref, smooth_ref, recv3).wait()
    for copy, reach in halo_copies:
        if reach is None:
            copy.wait_send()
        else:
            pl.when(reach)(copy.wait_send)
    most = pieces.at[pl.ds(0, GROUP - 1)]
    pltpu.make_async_copy(most, most, send1).wait()
    most = held.at[pl.ds(0, PLACES - 1)]
    pltpu.make_async_copy(most, most, send2).wait()
    most = smooth_ref.at[pl.ds(0, GROUP - 1)]
    pltpu.make_async_copy(most, most, send3).wait()


def body(displacement, earlier_field, region_ids, material, mode_shapes, band_edges):
    vmem = pl.BlockSpec(memory_space=pltpu.VMEM)
    smem = pl.BlockSpec(memory_space=pltpu.SMEM)
    dma = pltpu.SemaphoreType.DMA
    lanes = 2 * PADB
    shapes = mode_shapes.T
    final, smooth = pl.pallas_call(
        rail_kernel,
        out_shape=(
            jax.ShapeDtypeStruct((DEPTH, CELLS_HERE), jnp.float32),
            jax.ShapeDtypeStruct((GROUP, TILES, lanes), jnp.float32),
        ),
        in_specs=[vmem] * 3 + [smem] * 2 + [pl.BlockSpec(memory_space=pl.ANY)] * 7,
        out_specs=(vmem, vmem),
        scratch_shapes=[
            pltpu.VMEM((MODES, CELLS_HERE), jnp.float32),
            pltpu.VMEM(TABLES[0].shape[1:], jnp.float32),
            *[pltpu.VMEM(t.shape, jnp.float32) for t in TABLES[1:]],
            dma((7,)),
            pltpu.VMEM((DEPTH, EDGE), jnp.float32),
            pltpu.VMEM((PAD, CELLS_HERE), jnp.float32),
            pltpu.VMEM((2 * TALL + PAD, BROAD), jnp.float32),
            pltpu.VMEM((GROUP, TILES, lanes), jnp.float32),
            pltpu.VMEM((GROUP, TILES, lanes), jnp.float32),
            pltpu.VMEM((YS * TILES, lanes), jnp.float32),
            pltpu.VMEM((PLACES, YS * TILES, lanes), jnp.float32),
            pltpu.VMEM((YS, TILES, lanes), jnp.float32),
            dma((18,)), dma, dma, dma, dma, dma, dma, dma,
        ],
        compiler_params=pltpu.CompilerParams(collective_id=0, has_side_effects=True),
    )(
        displacement, earlier_field, region_ids.reshape(1, CELLS_HERE), material, band_edges,
        shapes, *[jnp.asarray(t) for t in TABLES],
    )
    return pl.pallas_call(
        finish_kernel,
        out_shape=(
            jax.ShapeDtypeStruct((DEPTH, CELLS_HERE), jnp.float32),
            jax.ShapeDtypeStruct((DEPTH, CELLS_HERE), jnp.bfloat16),
        ),
    )(final, smooth, shapes)


def solution(mesh):
    return jax.shard_map(
        body,
        mesh=mesh,
        in_specs=(P("slab", "sec"), P("slab", "sec"), P("sec"), P(), P("sec", None), P()),
        out_specs=(P("slab", "sec"), P("slab", "sec")),
        check_vma=False,
    )
```
